32 devices in a mesh: grp: 2 (over y), freq: 16 (over z, x, core).
Axes of the slice: x: 2, y: 2, z: 4, core: 2. Of those that a mesh axis runs over, the one named last changes fastest.
Arguments:
- source_field: bfloat16 [4, 16, 512, 256], P('grp', 'freq'), parts along dimension 0, may hold values from -6 to 6
- receiver_field: bfloat16 [4, 16, 512, 256], P('grp', 'freq'), parts along dimension 0, may hold values from -6 to 6
- slowness_slabs: bfloat16 [32, 768, 512], P(('grp', 'freq')), parts along dimension 0, may hold values from 0.3984375 to 1.1953125
- slab_map: int32 [4], P('grp'), parts along dimension 0, may hold values from 0 to 15
- reference_gaps: float32 [4, 3], P('grp'), parts along dimension 0, may hold values from 0.1 to 0.3
- reference_index: int32 [4, 512, 256], P('grp'), parts along dimension 0, may hold values from 0 to 1
- frequency_bins: int32 [16], replicated, may hold values from 10 to 120
- shot_corner: int32 [4], P('grp'), parts along dimension 0, may hold values from 0 to 256
Outputs:
- image: float32 [4, 512, 256, 256], P('grp', 'freq'), parts along dimension 0
The draws below stay inside these ranges and needn't reach their ends.
There are 2 independent parts, one for each index of `grp`. The reference program is written for one: setup_inputs(seed, part) draws one part's arguments, and reference() takes and returns one part's arrays. A program takes and returns all parts, laid end to end along the dimension named above; an argument that names none is the same for every part. Nothing has to cross between parts.
All inputs are finite; a program needn't handle non-finite values.
Results may differ from the reference program's by a relative error of at most 0.014.
Values may be sent and summed in bfloat16 or wider, within the bound.
A program may use at most 128 MiB of HBM per device.

```python
import math
import jax
import jax.numpy as jnp
from jax import lax

NX = 512
NY = 256
LAGS = 256
NREF = 3
DEPTHS = 2
SPAN = 256
NW = 16
SLABS = 16
MX = 768
MY = 512


def place_ends(values, key, smallest, high):
    dims = values.shape
    spot = [jax.random.randint(jax.random.fold_in(key, axis), (), 0, dims[axis]) for axis in range(len(dims))]
    values = values.at[tuple(spot)].set(smallest)
    longest = dims.index(max(dims))
    spot[longest] = (spot[longest] + 1) % dims[longest]
    return values.at[tuple(spot)].set(high)


def steps_of(key, dims, pieces, low, largest):
    level = 1.0
    for dim, blocks in pieces:
        steps = jax.random.uniform(jax.random.fold_in(jax.random.fold_in(key, 6), dim), (blocks,), jnp.float32, low / len(pieces), largest / len(pieces))
        level = level * jnp.repeat(jnp.exp(steps), dims[dim] // blocks).reshape((-1,) + (1,) * (len(dims) - 1 - dim))
    return level


def normal_values(stream_key, shape, spread, reach, shards=(), held_as=jnp.bfloat16):
    level = steps_of(stream_key, shape, shards, -0.22, 0.18) if shards else 1.0
    result = jax.random.normal(stream_key, shape, jnp.float32) * spread * level
    return jnp.minimum(jnp.maximum(result, -reach), reach).astype(held_as)


def setup_inputs(seed: int = 0, part: int = 0) -> dict:
    keys = jax.random.split(jax.random.key(seed), 9)
    part_splits = jax.random.split(jax.random.fold_in(keys[8], part), 9)
    source_field = normal_values(part_splits[0], (2, NW, NX, NY), 1.0, 6.0, ((1, 16),))
    receiver_field = normal_values(part_splits[1], (2, NW, NX, NY), 1.0, 6.0, ((1, 16),))
    slowness_slabs = jnp.clip(0.3984375 + 0.796875 * jax.random.uniform(part_splits[2], (SLABS, MX, MY), jnp.float32) ** steps_of(part_splits[2], (SLABS, MX, MY), ((0, 16),), -0.2, 0.2), 0.3984375, 1.1953125).astype(jnp.bfloat16)
    slab_map = jax.random.randint(part_splits[3], (DEPTHS,), 0, SLABS).astype(jnp.int32)
    reference_gaps = jnp.clip(jnp.exp(jax.random.uniform(part_splits[4], (DEPTHS, NREF), jnp.float32, math.log(0.1), math.log(0.3))), 0.1, 0.3)
    reference_index = place_ends(jax.random.randint(part_splits[5], (DEPTHS, NX, NY), 0, NREF - 1), jax.random.fold_in(part_splits[5], 1), 0, (NREF - 1) - 1).astype(jnp.int32)
    frequency_bins = place_ends(jax.random.randint(keys[6], (NW,), 10, 121), jax.random.fold_in(keys[6], 1), 10, 120).astype(jnp.int32)
    shot_corner = jax.random.randint(part_splits[7], (2,), 0, SPAN + 1).astype(jnp.int32)
    return {"source_field": source_field, "receiver_field": receiver_field, "slowness_slabs": slowness_slabs, "slab_map": slab_map, "reference_gaps": reference_gaps, "reference_index": reference_index, "frequency_bins": frequency_bins, "shot_corner": shot_corner}


cell_width = 0.0125
layer_thick = 0.0125
bin_hertz = 0.5
period_bins = 500
slow_base = 0.3

def transform_table(length, forward):
    grid_steps = jnp.arange(length, dtype=jnp.int32)
    phases = jnp.mod(grid_steps[:, None] * grid_steps[None, :], length).astype(jnp.float32)
    angles = phases * (2.0 * math.pi / length)
    norm_scale = 1.0 / math.sqrt(length)
    cosine = jnp.cos(angles) * norm_scale
    sine_part = jnp.sin(angles) * norm_scale
    if forward:
        cross_term = -sine_part
    else:
        cross_term = sine_part
    return jnp.stack([jnp.stack([cosine, cross_term]), jnp.stack([-cross_term, cosine])]).astype(jnp.bfloat16)

def wave_numbers(length):
    grid_steps = jnp.arange(length, dtype=jnp.int32)
    folded = jnp.where(grid_steps < length // 2, grid_steps, grid_steps - length).astype(jnp.float32)
    return folded * (2.0 * math.pi / (length * cell_width))

def lag_table(frequency_bins, lag_count):
    offsets = jnp.arange(lag_count, dtype=jnp.int32) - lag_count // 2
    cycles = jnp.mod(frequency_bins[:, None] * offsets[None, :], period_bins).astype(jnp.float32)
    angles = cycles * (2.0 * math.pi / period_bins)
    return jnp.stack([jnp.cos(angles), -jnp.sin(angles)]).astype(jnp.bfloat16)

def phase_factors(angular, references, squares):
    radicand = (angular * references[:, None, None]) ** 2 - squares[None]
    vertical = jnp.sqrt(jnp.maximum(radicand, 0.0))
    fading = jnp.exp(-jnp.sqrt(jnp.maximum(-radicand, 0.0)) * layer_thick)
    return (fading * jnp.cos(vertical * layer_thick), fading * jnp.sin(vertical * layer_thick))

def rotate(field_pair, turn_angle):
    return jnp.stack([jnp.cos(turn_angle) * field_pair[0] - jnp.sin(turn_angle) * field_pair[1], jnp.cos(turn_angle) * field_pair[1] + jnp.sin(turn_angle) * field_pair[0]])

def extrapolate(field, angular, slowness, references, bracket, direction, tables, squares):
    forward_x, forward_y, inverse_x, inverse_y = tables
    half_done = jnp.einsum('cxy,cdyk->dxk', field.astype(jnp.float32), forward_y).astype(jnp.bfloat16)
    spectrum = jnp.einsum('cdxk,cxy->dky', forward_x, half_done.astype(jnp.float32))
    cos_part, sin_part = phase_factors(angular, references, squares)
    sin_part = direction * sin_part
    shifted = jnp.stack([cos_part * spectrum[0] - sin_part * spectrum[1], cos_part * spectrum[1] + sin_part * spectrum[0]], axis=1).astype(jnp.bfloat16)
    returned = jnp.einsum('cdxk,jcxy->jdky', inverse_x, shifted.astype(jnp.float32)).astype(jnp.bfloat16)
    refocused = jnp.einsum('jcxy,cdyk->jdxk', returned.astype(jnp.float32), inverse_y)
    lower_pair = bracket == 0
    lower_field = jnp.where(lower_pair[None], refocused[0], refocused[1])
    upper_field = jnp.where(lower_pair[None], refocused[1], refocused[2])
    slow_low = jnp.where(lower_pair, references[0], references[1])
    slow_high = jnp.where(lower_pair, references[1], references[2])
    weight = jnp.clip((slowness - slow_low) / (slow_high - slow_low), 0.0, 1.0)
    turn_low = direction * angular * layer_thick * (slowness - slow_low)
    turn_high = direction * angular * layer_thick * (slowness - slow_high)
    mixed = (1.0 - weight) * rotate(lower_field, turn_low) + weight * rotate(upper_field, turn_high)
    return mixed.astype(jnp.bfloat16)

def reference(source_field, receiver_field, slowness_slabs, slab_map, reference_gaps, reference_index, frequency_bins, shot_corner):
    tables = (transform_table(NX, True).astype(jnp.float32), transform_table(NY, True).astype(jnp.float32), transform_table(NX, False).astype(jnp.float32), transform_table(NY, False).astype(jnp.float32))
    wave_x = wave_numbers(NX)
    wave_y = wave_numbers(NY)
    squares = wave_x[:, None] ** 2 + wave_y[None, :] ** 2
    omegas = frequency_bins.astype(jnp.float32) * (2.0 * math.pi * bin_hertz)
    slow_list = []
    ref_list = []
    for depth_step in range(DEPTHS):
        slab = lax.dynamic_index_in_dim(slowness_slabs, slab_map[depth_step].astype(jnp.int32), 0, keepdims=False)
        window = lax.dynamic_slice(slab, (shot_corner[0].astype(jnp.int32), shot_corner[1].astype(jnp.int32)), (NX, NY))
        slow_list.append(window.astype(jnp.float32))
        ref_list.append(slow_base + jnp.cumsum(reference_gaps[depth_step]))

    def one_frequency(inputs):
        source, receiver, angular = inputs
        crosses = []
        for depth_step in range(DEPTHS):
            source = extrapolate(source, angular, slow_list[depth_step], ref_list[depth_step], reference_index[depth_step], 1.0, tables, squares)
            receiver = extrapolate(receiver, angular, slow_list[depth_step], ref_list[depth_step], reference_index[depth_step], -1.0, tables, squares)
            src_values = source.astype(jnp.float32)
            rec_values = receiver.astype(jnp.float32)
            real_part = src_values[0] * rec_values[0] + src_values[1] * rec_values[1]
            imag_part = src_values[0] * rec_values[1] - src_values[1] * rec_values[0]
            crosses.append(jnp.stack([real_part, imag_part]).astype(jnp.bfloat16))
        return jnp.stack(crosses)
    crosses = lax.map(one_frequency, (jnp.moveaxis(source_field, 1, 0), jnp.moveaxis(receiver_field, 1, 0), omegas))
    lag_weights = lag_table(frequency_bins, LAGS).astype(jnp.float32)
    images = []
    for depth_step in range(DEPTHS):
        summed = jnp.einsum('wcxy,cwl->xyl', crosses[:, depth_step].astype(jnp.float32), lag_weights)
        images.append(summed * NW ** (-0.5))
    return jnp.stack(images)
```

```python
import functools
import math

import jax
import jax.numpy as jnp
import numpy as np
from jax import lax
from jax.experimental import pallas as pl
from jax.experimental.pallas import tpu as pltpu
from jax.sharding import PartitionSpec as P

LAGS = 256

cell_width = 0.0125
layer_thick = 0.0125
bin_hertz = 0.5
period_bins = 500
slow_base = 0.3
chunk = 16
tile = 256


def transform_block(length):
    steps = np.arange(length, dtype=np.int64)
    phases = np.mod(steps[:, None] * steps[None, :], length).astype(np.float32)
    angles = phases * np.float32(2.0 * math.pi / length)
    scale = np.float32(1.0 / math.sqrt(length))
    cosine = np.cos(angles) * scale
    sine = np.sin(angles) * scale
    return np.block([[cosine, -sine], [sine, cosine]]).astype(jnp.bfloat16)


def lag_table(frequency_bins, lag_count):
    offsets = jnp.arange(lag_count, dtype=jnp.int32) - lag_count // 2
    cycles = jnp.mod(frequency_bins[:, None] * offsets[None, :], period_bins).astype(jnp.float32)
    angles = cycles * (2.0 * math.pi / period_bins)
    return jnp.stack([jnp.cos(angles), -jnp.sin(angles)]).astype(jnp.bfloat16)


def sin_cos(angle):
    turns = jnp.floor(angle * (2.0 / math.pi) + 0.5)
    rest = angle - turns * 1.5707855224609375
    rest = rest - turns * 1.0804334124e-05
    quarter = turns.astype(jnp.int32)
    square = rest * rest
    sine = rest + rest * square * (
        -1.6666654611e-1 + square * (8.3321608736e-3 + square * -1.9515295891e-4)
    )
    cosine = (
        1.0
        - 0.5 * square
        + square * square
        * (4.166664568298827e-2 + square * (-1.388731625493765e-3 + square * 2.443315711809948e-5))
    )
    odd = (quarter & 1) == 1
    sine_out = jnp.where(odd, cosine, sine)
    cosine_out = jnp.where(odd, sine, cosine)
    sine_out = jnp.where((quarter & 2) == 2, -sine_out, sine_out)
    cosine_out = jnp.where(((quarter + 1) & 2) == 2, -cosine_out, cosine_out)
    return sine_out, cosine_out


def folded_square(index, length):
    folded = jnp.where(index < length // 2, index, index - length).astype(jnp.float32)
    wave = folded * (2.0 * math.pi / (length * cell_width))
    return wave * wave


def step_kernel(
    scalars, source, receiver, table_x, table_y, slow, bracket,
    out_source, out_receiver, cross,
    half, spectrum, shifted, returned, refocused,
):
    rows_x, cols_y = slow.shape
    angular = scalars[0]
    fields = (source, receiver)
    signs = (1.0, -1.0)

    def lanes(which):
        return pl.ds(which * cols_y, cols_y)

    for which, field in enumerate(fields):
        for start in range(0, rows_x, tile):
            rows = pl.ds(start, tile)
            both = jnp.concatenate([field[0, rows, :], field[1, rows, :]], axis=1)
            out = jnp.dot(both, table_y[...], preferred_element_type=jnp.float32)
            out = out.astype(jnp.bfloat16)
            half[rows, lanes(which)] = out[:, :cols_y]
            half[pl.ds(rows_x + start, tile), lanes(which)] = out[:, cols_y:]

    @pl.loop(0, 2 * rows_x // tile)
    def _(number):
        rows = pl.ds(pl.multiple_of(number * tile, tile), tile)
        spectrum[rows, :] = jnp.dot(
            table_x[rows, :], half[...], preferred_element_type=jnp.float32
        )

    for ref in range(3):
        @pl.loop(0, rows_x // chunk)
        def _(number):
            start = pl.multiple_of(number * chunk, chunk)
            rows = pl.ds(start, chunk)
            low_rows = pl.ds(rows_x + start, chunk)
            row_index = lax.broadcasted_iota(jnp.int32, (chunk, cols_y), 0) + start
            col_index = lax.broadcasted_iota(jnp.int32, (chunk, cols_y), 1)
            squares = folded_square(row_index, rows_x) + folded_square(col_index, cols_y)
            reach = angular * scalars[1 + ref]
            radicand = reach * reach - squares
            depth = jnp.sqrt(jnp.abs(radicand)) * layer_thick
            moving = radicand > 0.0
            fading = jnp.exp(jnp.where(moving, 0.0, -depth))
            sine, cosine = sin_cos(jnp.where(moving, depth, 0.0) - reach * layer_thick)
            cosine = fading * cosine
            sine = fading * sine
            for which in range(2):
                turned = signs[which] * sine
                real = spectrum[rows, lanes(which)]
                imag = spectrum[low_rows, lanes(which)]
                shifted[rows, lanes(which)] = (cosine * real - turned * imag).astype(jnp.bfloat16)
                shifted[low_rows, lanes(which)] = (-(cosine * imag + turned * real)).astype(
                    jnp.bfloat16
                )

        @pl.loop(0, 2 * rows_x // tile)
        def _(number):
            rows = pl.ds(pl.multiple_of(number * tile, tile), tile)
            returned[rows, :] = jnp.dot(
                table_x[rows, :], shifted[...], preferred_element_type=jnp.float32
            ).astype(jnp.bfloat16)

        for which in range(2):
            for start in range(0, rows_x, tile):
                rows = pl.ds(start, tile)
                both = jnp.concatenate(
                    [
                        returned[rows, lanes(which)],
                        returned[pl.ds(rows_x + start, tile), lanes(which)],
                    ],
                    axis=1,
                )
                refocused[ref, which, rows, :] = jnp.dot(
                    both, table_y[...], preferred_element_type=jnp.float32
                )

    @pl.loop(0, rows_x // chunk)
    def _(number):
        rows = pl.ds(pl.multiple_of(number * chunk, chunk), chunk)
        slowness = slow[rows, :].astype(jnp.float32)
        lower = bracket[rows, :] == 0
        slow_low = jnp.where(lower, scalars[1], scalars[2])
        slow_gap = jnp.where(lower, scalars[4], scalars[5])
        weight = jnp.clip((slowness - slow_low) / slow_gap, 0.0, 1.0)
        sine, cosine = sin_cos((angular * layer_thick) * slowness)
        rounded = []
        for which, out in enumerate((out_source, out_receiver)):
            mixed = []
            for part in range(2):
                first = refocused[0, which, rows, lanes(part)]
                second = refocused[1, which, rows, lanes(part)]
                third = refocused[2, which, rows, lanes(part)]
                low = jnp.where(lower, first, second)
                high = jnp.where(lower, second, third)
                mixed.append((1.0 - weight) * low + weight * high)
            turned = signs[which] * sine
            real = (cosine * mixed[0] + turned * mixed[1]).astype(jnp.bfloat16)
            imag = (turned * mixed[0] - cosine * mixed[1]).astype(jnp.bfloat16)
            out[0, rows, :] = real
            out[1, rows, :] = imag
            rounded.append((real.astype(jnp.float32), imag.astype(jnp.float32)))
        (sr, si), (rr, ri) = rounded
        cross[0, rows, :] = (sr * rr + si * ri).astype(jnp.bfloat16)
        cross[1, rows, :] = (sr * ri - si * rr).astype(jnp.bfloat16)


def depth_step(scalars, source, receiver, table_x, table_y, slow, bracket):
    rows_x, cols_y = slow.shape
    field = jax.ShapeDtypeStruct((2, rows_x, cols_y), jnp.bfloat16)
    vmem = pl.BlockSpec(memory_space=pltpu.VMEM)
    flops = 2 * 4 * (2 * rows_x) * (2 * rows_x + 2 * cols_y) * 2 * cols_y
    return pl.pallas_call(
        step_kernel,
        out_shape=(field, field, field),
        in_specs=[pl.BlockSpec(memory_space=pltpu.SMEM)] + [vmem] * 6,
        out_specs=(vmem,) * 3,
        scratch_shapes=[
            pltpu.VMEM((2 * rows_x, 2 * cols_y), jnp.bfloat16),
            pltpu.VMEM((2 * rows_x, 2 * cols_y), jnp.float32),
            pltpu.VMEM((2 * rows_x, 2 * cols_y), jnp.bfloat16),
            pltpu.VMEM((2 * rows_x, 2 * cols_y), jnp.bfloat16),
            pltpu.VMEM((3, 2, rows_x, 2 * cols_y), jnp.float32),
        ],
        cost_estimate=pl.CostEstimate(
            flops=3 * flops, bytes_accessed=8 * 1024 * 1024, transcendentals=0
        ),
        compiler_params=pltpu.CompilerParams(vmem_limit_bytes=40 * 1024 * 1024),
    )(scalars, source, receiver, table_x, table_y, slow, bracket)


def share_kernel(devices, mine, out, pair, part, parts, total, pair_sems, send_sems, recv_sems):
    chips = devices // 2
    me = lax.axis_index("freq")
    grp = lax.axis_index("grp")
    core = lax.rem(me, 2)
    chip = me // 2
    other = 1 - core

    def device(where, side):
        return (grp, where * 2 + side)

    barrier = pltpu.get_barrier_semaphore()
    pl.semaphore_signal(
        barrier, inc=1, device_id=device(chip, other), device_id_type=pl.DeviceIdType.MESH
    )
    for hop in range(1, chips):
        pl.semaphore_signal(
            barrier, inc=1, device_id=device(lax.rem(chip + hop, chips), core),
            device_id_type=pl.DeviceIdType.MESH,
        )
    pl.semaphore_wait(barrier, chips)

    def copy(source, target, send, recv, where, side):
        return pltpu.make_async_remote_copy(
            src_ref=source, dst_ref=target, send_sem=send, recv_sem=recv,
            device_id=device(where, side), device_id_type=pl.DeviceIdType.MESH,
        )

    first = copy(mine.at[other], pair, pair_sems.at[0], pair_sems.at[1], chip, other)
    first.start()
    first.wait()
    part[...] = mine[core] + pair[...]
    sends = []
    for hop in range(1, chips):
        to = lax.rem(chip + hop, chips)
        sends.append(
            copy(part.at[to], parts.at[hop], send_sems.at[0, hop], recv_sems.at[0, hop], to, core)
        )
        sends[-1].start()
    summed = part[chip]
    for hop in range(1, chips):
        sends[hop - 1].wait()
        summed = summed + parts[hop]
    total[...] = summed
    out[core, chip] = summed
    sends = []
    for hop in range(1, chips):
        to = lax.rem(chip + hop, chips)
        sends.append(
            copy(
                total, out.at[core, chip], send_sems.at[1, hop], recv_sems.at[1, hop], to, core
            )
        )
        sends[-1].start()
    for each in sends:
        each.wait()
    last = copy(out.at[core], out.at[core], pair_sems.at[2], pair_sems.at[3], chip, other)
    last.start()
    last.wait()


def share(blocks, devices):
    chips = devices // 2
    whole = blocks.shape
    rows = math.prod(whole[:-1]) // devices
    held = (2, chips, rows, whole[-1])
    vmem = pl.BlockSpec(memory_space=pltpu.VMEM)
    shared = pl.pallas_call(
        functools.partial(share_kernel, devices),
        out_shape=jax.ShapeDtypeStruct(held, blocks.dtype),
        in_specs=[vmem],
        out_specs=vmem,
        scratch_shapes=[
            pltpu.VMEM(held[1:], blocks.dtype),
            pltpu.VMEM(held[1:], blocks.dtype),
            pltpu.VMEM(held[1:], blocks.dtype),
            pltpu.VMEM(held[2:], blocks.dtype),
            pltpu.SemaphoreType.DMA((4,)),
            pltpu.SemaphoreType.DMA((2, chips)),
            pltpu.SemaphoreType.DMA((2, chips)),
        ],
        compiler_params=pltpu.CompilerParams(collective_id=0, has_side_effects=True),
    )(blocks.reshape(held))
    return shared.reshape(whole)


def shards(
    devices,
    source_field,
    receiver_field,
    slowness_slabs,
    slab_map,
    reference_gaps,
    reference_index,
    frequency_bins,
    shot_corner,
):
    rows_x = source_field.shape[2]
    cols_y = source_field.shape[3]
    depths = slab_map.shape[0]
    table_x = jnp.asarray(transform_block(rows_x).T)
    table_y = jnp.asarray(transform_block(cols_y))
    freq_rank = lax.axis_index("freq")
    slab_count = slowness_slabs.shape[0]
    angular = lax.dynamic_index_in_dim(frequency_bins, freq_rank, 0, False).astype(
        jnp.float32
    ) * (2.0 * math.pi * bin_hertz)
    lag_weights = lag_table(frequency_bins, LAGS)
    windows = []
    for depth in range(depths):
        slab = slab_map[depth]
        window = lax.dynamic_slice(
            slowness_slabs,
            (slab % slab_count, shot_corner[0], shot_corner[1]),
            (1, rows_x, cols_y),
        )[0]
        windows.append(jnp.where(slab // slab_count == freq_rank, window, 0))
    slow = share(jnp.stack(windows), devices)
    source = source_field[:, 0]
    receiver = receiver_field[:, 0]
    images = []
    scale = frequency_bins.shape[0] ** (-0.5)
    crosses = []
    for depth in range(depths):
        references = slow_base + jnp.cumsum(reference_gaps[depth])
        scalars = jnp.concatenate([angular[None], references, references[1:] - references[:-1]])
        source, receiver, cross = depth_step(
            scalars, source, receiver, table_x, table_y, slow[depth], reference_index[depth]
        )
        crosses.append(
            lax.all_to_all(cross[:, None], "freq", split_axis=2, concat_axis=1, tiled=True)
        )
    return (
        jnp.einsum(
            "dcwab,cwl->dabl", jnp.stack(crosses), lag_weights, preferred_element_type=jnp.float32
        )
        * scale
    )


def solution(mesh):
    placed = (
        P("grp", "freq", None, None),
        P("grp", "freq", None, None),
        P(("grp", "freq"), None, None),
        P("grp"),
        P("grp", None),
        P("grp", None, None),
        P(),
        P("grp"),
    )
    return jax.shard_map(
        functools.partial(shards, mesh.shape["freq"]),
        mesh=mesh,
        in_specs=placed,
        out_specs=P("grp", "freq", None, None),
        check_vma=False,
    )
```

```python
import functools
import math

import jax
import jax.numpy as jnp
import numpy as np
from jax import lax
from jax.experimental import pallas as pl
from jax.experimental.pallas import tpu as pltpu
from jax.sharding import PartitionSpec as P

LAGS = 256

cell_width = 0.0125
layer_thick = 0.0125
bin_hertz = 0.5
period_bins = 500
slow_base = 0.3
chunk = 16
tile = 256


def spectral_order(length):
    half = length // 2
    return np.concatenate([np.arange(half), [half], np.arange(length - 1, half, -1)])


def parts_of(length):
    steps = np.arange(length, dtype=np.int64)
    phases = np.mod(steps[:, None] * steps[None, :], length).astype(np.float32)
    angles = phases * np.float32(2.0 * math.pi / length)
    scale = np.float32(1.0 / math.sqrt(length))
    return np.cos(angles) * scale, np.sin(angles) * scale


def transform_block(length):
    cosine, sine = parts_of(length)
    return np.block([[cosine, -sine], [sine, cosine]]).astype(jnp.bfloat16)


def transform_pair(length):
    cosine, sine = parts_of(length)
    order = spectral_order(length)
    return (
        np.concatenate([cosine[order], sine[order]], axis=1).astype(jnp.bfloat16),
        np.concatenate([cosine[:, order], sine[:, order]], axis=1).astype(jnp.bfloat16),
    )


def lag_table(frequency_bins, lag_count):
    offsets = jnp.arange(lag_count, dtype=jnp.int32) - lag_count // 2
    cycles = jnp.mod(frequency_bins[:, None] * offsets[None, :], period_bins).astype(jnp.float32)
    angles = cycles * (2.0 * math.pi / period_bins)
    return jnp.stack([jnp.cos(angles), -jnp.sin(angles)]).astype(jnp.bfloat16)


def sin_cos(angle):
    turns = jnp.floor(angle * (2.0 / math.pi) + 0.5)
    rest = angle - turns * 1.5707855224609375
    rest = rest - turns * 1.0804334124e-05
    quarter = turns.astype(jnp.int32)
    square = rest * rest
    sine = rest + rest * square * (
        -1.6666654611e-1 + square * (8.3321608736e-3 + square * -1.9515295891e-4)
    )
    cosine = (
        1.0
        - 0.5 * square
        + square * square
        * (4.166664568298827e-2 + square * (-1.388731625493765e-3 + square * 2.443315711809948e-5))
    )
    odd = (quarter & 1) == 1
    sine_out = jnp.where(odd, cosine, sine)
    cosine_out = jnp.where(odd, sine, cosine)
    sine_out = jnp.where((quarter & 2) == 2, -sine_out, sine_out)
    cosine_out = jnp.where(((quarter + 1) & 2) == 2, -cosine_out, cosine_out)
    return sine_out, cosine_out


def window_kernel(
    devices, scalars, source, receiver, table_f, table_i, table_y, windows, bracket,
    received,
    half, spectrum, shifted_a, shifted_b, returned, refocused, fields, cross,
    pair, part, parts, total, slow,
    pair_sems, scatter_sems, gather_sems, cross_sems,
):
    depths, rows_x, cols_y = bracket.shape
    chips = devices // 2
    me = lax.axis_index("freq")
    grp = lax.axis_index("grp")
    core = lax.rem(me, 2)
    chip = me // 2
    other = 1 - core
    share_rows = rows_x // devices
    signs = (1.0, -1.0)
    middle = rows_x // 2

    def lanes(which):
        return pl.ds(which * cols_y, cols_y)

    def remote(source_ref, target_ref, sems, place):
        return pltpu.make_async_remote_copy(
            src_ref=source_ref, dst_ref=target_ref, send_sem=sems[0], recv_sem=sems[1],
            device_id=(grp, place), device_id_type=pl.DeviceIdType.MESH,
        )

    def hop_to(hop):
        return lax.rem(chip + hop, chips)

    def swap_first(d):
        return remote(
            windows.at[d, other], pair.at[d], (pair_sems.at[d, 0], pair_sems.at[d, 1]),
            chip * 2 + other,
        )

    def scatter(d, hop):
        return remote(
            part.at[d, hop_to(hop)], parts.at[d, hop],
            (scatter_sems.at[d, 0, hop], scatter_sems.at[d, 1, hop]), hop_to(hop) * 2 + core,
        )

    def gather(d, hop):
        return remote(
            total.at[d], slow.at[d, core, chip],
            (gather_sems.at[d, 0, hop], gather_sems.at[d, 1, hop]), hop_to(hop) * 2 + core,
        )

    def swap_last(d):
        return remote(
            slow.at[d, core], slow.at[d, core], (pair_sems.at[d, 2], pair_sems.at[d, 3]),
            chip * 2 + other,
        )

    def send_cross(d, hop):
        to = lax.rem(me + hop, devices)
        return remote(
            cross.at[d, to], received.at[d, me],
            (cross_sems.at[d, 0, hop], cross_sems.at[d, 1, hop]), to,
        )

    def begin_scatter(d):
        swap_first(d).wait()
        part[d] = windows[d, core] + pair[d]

        @pl.loop(1, chips)
        def _(hop):
            scatter(d, hop).start()

    def begin_gather(d):
        @pl.loop(1, chips)
        def _(hop):
            scatter(d, hop).wait()

        summed = part[d, chip]
        for hop in range(1, chips):
            summed = summed + parts[d, hop]
        total[d] = summed
        slow[d, core, chip] = summed

        @pl.loop(1, chips)
        def _(hop):
            gather(d, hop).start()

    def begin_last(d):
        @pl.loop(1, chips)
        def _(hop):
            gather(d, hop).wait()

        swap_last(d).start()

    barrier = pltpu.get_barrier_semaphore()

    @pl.loop(1, devices)
    def _(hop):
        pl.semaphore_signal(
            barrier, inc=1, device_id=(grp, lax.rem(me + hop, devices)),
            device_id_type=pl.DeviceIdType.MESH,
        )

    pl.semaphore_wait(barrier, devices - 1)
    for d in range(depths):
        swap_first(d).start()

    columns = lax.broadcasted_iota(jnp.int32, (chunk, cols_y), 1)
    wave_y = jnp.where(columns < cols_y // 2, columns, cols_y - columns).astype(jnp.float32) * (
        2.0 * math.pi / (cols_y * cell_width)
    )
    squares_y = wave_y * wave_y

    def phases(d, ref, magnitude):
        wave_x = magnitude.astype(jnp.float32) * (2.0 * math.pi / (rows_x * cell_width))
        reach = scalars[d, 0] * scalars[d, 1 + ref]
        radicand = reach * reach - (wave_x * wave_x + squares_y)
        depth = jnp.sqrt(jnp.abs(radicand)) * layer_thick
        moving = radicand > 0.0
        fading = jnp.exp(jnp.where(moving, 0.0, -depth))
        sine, cosine = sin_cos(jnp.where(moving, depth, 0.0) - reach * layer_thick)
        return fading * cosine, fading * sine

    def apply_phase(target, cosine, sine, start):
        rows = pl.ds(start, chunk)
        low_rows = pl.ds(rows_x + start, chunk)
        for which in range(2):
            turned = signs[which] * sine
            real = spectrum[rows, lanes(which)]
            imag = spectrum[low_rows, lanes(which)]
            new_real = (cosine * real - turned * imag).astype(jnp.bfloat16)
            target[rows, lanes(which)] = new_real
            target[low_rows, lanes(which)] = (-(cosine * imag + turned * real)).astype(jnp.bfloat16)
            target[pl.ds(2 * rows_x + start, chunk), lanes(which)] = -new_real

    counted = lax.broadcasted_iota(jnp.int32, (chunk, cols_y), 0)

    def shift_chunk(d, ref, target, start):
        cosine, sine = phases(d, ref, counted + start)
        apply_phase(target, cosine, sine, start)
        apply_phase(target, cosine, sine, pl.multiple_of(middle + start, chunk))

    def shift_edge(d, ref, target):
        cosine, sine = phases(d, ref, jnp.where(counted == 0, middle, counted))
        apply_phase(target, cosine, sine, middle)

    def multiply(table, values, rows):
        block = table[rows, :]
        real = jnp.dot(block, values[: 2 * rows_x, :], preferred_element_type=jnp.float32)
        imag = jnp.dot(block, values[rows_x:, :], preferred_element_type=jnp.float32)
        return real, imag

    def slow_rows(d, start):
        if share_rows >= chunk:
            block = start // share_rows
            inner = pl.multiple_of(lax.rem(start, share_rows), chunk)
            return slow[d, block // chips, lax.rem(block, chips), pl.ds(inner, chunk), :].astype(
                jnp.float32
            )
        pieces = []
        for piece in range(chunk // share_rows):
            block = start // share_rows + piece
            pieces.append(
                slow[d, block // chips, lax.rem(block, chips)].astype(jnp.float32)
            )
        return jnp.concatenate(pieces, axis=0)

    def store_cross(d, start, which, values):
        if share_rows >= chunk:
            inner = pl.multiple_of(lax.rem(start, share_rows), chunk)
            cross[d, start // share_rows, which, pl.ds(inner, chunk), :] = values.astype(
                jnp.bfloat16
            )
        else:
            for piece in range(chunk // share_rows):
                cross[d, start // share_rows + piece, which] = values[
                    piece * share_rows : (piece + 1) * share_rows
                ].astype(jnp.bfloat16)

    for d in range(depths):
        for which, field in enumerate((source, receiver) if d == 0 else (fields.at[0], fields.at[1])):
            for start in range(0, rows_x, tile):
                rows = pl.ds(start, tile)
                both = jnp.concatenate([field[0, rows, :], field[1, rows, :]], axis=1)
                out = jnp.dot(both, table_y[...], preferred_element_type=jnp.float32)
                out = out.astype(jnp.bfloat16)
                half[rows, lanes(which)] = out[:, :cols_y]
                half[pl.ds(rows_x + start, tile), lanes(which)] = out[:, cols_y:]
                half[pl.ds(2 * rows_x + start, tile), lanes(which)] = -out[:, :cols_y]
        if d == 0:
            begin_scatter(0)

        @pl.loop(0, rows_x // tile)
        def _(number):
            start = pl.multiple_of(number * tile, tile)
            real, imag = multiply(table_f, half, pl.ds(start, tile))
            spectrum[pl.ds(start, tile), :] = real
            spectrum[pl.ds(rows_x + start, tile), :] = imag

        if d == 0:
            begin_gather(0)
            for later in range(1, depths):
                begin_scatter(later)

        @pl.loop(0, middle // chunk)
        def _(number):
            shift_chunk(d, 0, shifted_a, pl.multiple_of(number * chunk, chunk))

        shift_edge(d, 0, shifted_a)
        for ref in range(3):
            now, later_shift = (shifted_a, shifted_b) if ref % 2 == 0 else (shifted_b, shifted_a)
            per_tile = middle // chunk // (rows_x // tile)

            @pl.loop(0, rows_x // tile)
            def _(number):
                start = pl.multiple_of(number * tile, tile)
                real, imag = multiply(table_i, now, pl.ds(start, tile))
                returned[pl.ds(start, tile), :] = real.astype(jnp.bfloat16)
                returned[pl.ds(rows_x + start, tile), :] = imag.astype(jnp.bfloat16)
                if ref < 2:
                    for each in range(per_tile):
                        shift_chunk(
                            d, ref + 1, later_shift,
                            pl.multiple_of((number * per_tile + each) * chunk, chunk),
                        )

            if ref < 2:
                shift_edge(d, ref + 1, later_shift)
            for which in range(2):
                for start in range(0, rows_x, tile):
                    rows = pl.ds(start, tile)
                    both = jnp.concatenate(
                        [
                            returned[rows, lanes(which)],
                            returned[pl.ds(rows_x + start, tile), lanes(which)],
                        ],
                        axis=1,
                    )
                    refocused[ref, which, rows, :] = jnp.dot(
                        both, table_y[...], preferred_element_type=jnp.float32
                    )
            if d == 0 and ref == 0:
                begin_last(0)
                for later in range(1, depths):
                    begin_gather(later)
            if d == 0 and ref == 1:
                for later in range(1, depths):
                    begin_last(later)
        if d == 0:
            for each in range(depths):
                swap_last(each).wait()

        @pl.loop(0, rows_x // chunk)
        def _(number):
            start = pl.multiple_of(number * chunk, chunk)
            rows = pl.ds(start, chunk)
            slowness = slow_rows(d, start)
            lower = bracket[d, rows, :] == 0
            slow_low = jnp.where(lower, scalars[d, 1], scalars[d, 2])
            slow_gap = jnp.where(lower, scalars[d, 4], scalars[d, 5])
            weight = jnp.clip((slowness - slow_low) / slow_gap, 0.0, 1.0)
            sine, cosine = sin_cos((scalars[d, 0] * layer_thick) * slowness)
            rounded = []
            for which in range(2):
                mixed = []
                for side in range(2):
                    first = refocused[0, which, rows, lanes(side)]
                    second = refocused[1, which, rows, lanes(side)]
                    third = refocused[2, which, rows, lanes(side)]
                    low = jnp.where(lower, first, second)
                    high = jnp.where(lower, second, third)
                    mixed.append((1.0 - weight) * low + weight * high)
                turned = signs[which] * sine
                real = (cosine * mixed[0] + turned * mixed[1]).astype(jnp.bfloat16)
                imag = (turned * mixed[0] - cosine * mixed[1]).astype(jnp.bfloat16)
                if d < depths - 1:
                    fields[which, 0, rows, :] = real
                    fields[which, 1, rows, :] = imag
                rounded.append((real.astype(jnp.float32), imag.astype(jnp.float32)))
            (sr, si), (rr, ri) = rounded
            store_cross(d, start, 0, sr * rr + si * ri)
            store_cross(d, start, 1, sr * ri - si * rr)

        @pl.loop(1, devices)
        def _(hop):
            send_cross(d, hop).start()

        received[d, me] = cross[d, me]
    for d in range(depths):
        @pl.loop(1, devices)
        def _(hop):
            send_cross(d, hop).wait()


def cross_spectra(devices, scalars, source, receiver, windows, bracket):
    depths, rows_x, cols_y = bracket.shape
    chips = devices // 2
    share_rows = rows_x // devices
    table_f, table_i = transform_pair(rows_x)
    vmem = pl.BlockSpec(memory_space=pltpu.VMEM)
    flops = 16 * rows_x * (2 * rows_x + 2 * cols_y) * 2 * cols_y * depths
    dma = pltpu.SemaphoreType.DMA
    held = (depths, chips, share_rows, cols_y)
    return pl.pallas_call(
        functools.partial(window_kernel, devices),
        out_shape=jax.ShapeDtypeStruct((depths, devices, 2, share_rows, cols_y), jnp.bfloat16),
        in_specs=[pl.BlockSpec(memory_space=pltpu.SMEM)] + [vmem] * 7,
        out_specs=vmem,
        scratch_shapes=[
            pltpu.VMEM((3 * rows_x, 2 * cols_y), jnp.bfloat16),
            pltpu.VMEM((2 * rows_x, 2 * cols_y), jnp.float32),
            pltpu.VMEM((3 * rows_x, 2 * cols_y), jnp.bfloat16),
            pltpu.VMEM((3 * rows_x, 2 * cols_y), jnp.bfloat16),
            pltpu.VMEM((2 * rows_x, 2 * cols_y), jnp.bfloat16),
            pltpu.VMEM((3, 2, rows_x, 2 * cols_y), jnp.float32),
            pltpu.VMEM((2, 2, rows_x, cols_y), jnp.bfloat16),
            pltpu.VMEM((depths, devices, 2, share_rows, cols_y), jnp.bfloat16),
            pltpu.VMEM(held, jnp.bfloat16),
            pltpu.VMEM(held, jnp.bfloat16),
            pltpu.VMEM(held, jnp.bfloat16),
            pltpu.VMEM((depths, share_rows, cols_y), jnp.bfloat16),
            pltpu.VMEM((depths, 2, chips, share_rows, cols_y), jnp.bfloat16),
            dma((depths, 4)),
            dma((depths, 2, chips)),
            dma((depths, 2, chips)),
            dma((depths, 2, devices)),
        ],
        cost_estimate=pl.CostEstimate(
            flops=4 * flops, bytes_accessed=8 * 1024 * 1024, transcendentals=0
        ),
        compiler_params=pltpu.CompilerParams(
            collective_id=0, has_side_effects=True, vmem_limit_bytes=56 * 1024 * 1024
        ),
    )(
        scalars, source, receiver, jnp.asarray(table_f), jnp.asarray(table_i),
        jnp.asarray(transform_block(cols_y)),
        windows.reshape(depths, 2, chips, share_rows, cols_y), bracket,
    )


def shards(
    devices,
    source_field,
    receiver_field,
    slowness_slabs,
    slab_map,
    reference_gaps,
    reference_index,
    frequency_bins,
    shot_corner,
):
    rows_x = source_field.shape[2]
    cols_y = source_field.shape[3]
    depths = slab_map.shape[0]
    freq_rank = lax.axis_index("freq")
    slab_count = slowness_slabs.shape[0]
    angular = lax.dynamic_index_in_dim(frequency_bins, freq_rank, 0, False).astype(
        jnp.float32
    ) * (2.0 * math.pi * bin_hertz)
    lag_weights = lag_table(frequency_bins, LAGS)
    windows = []
    for depth in range(depths):
        slab = slab_map[depth]
        window = lax.dynamic_slice(
            slowness_slabs,
            (slab % slab_count, shot_corner[0], shot_corner[1]),
            (1, rows_x, cols_y),
        )[0]
        windows.append(jnp.where(slab // slab_count == freq_rank, window, 0))
    references = slow_base + jnp.cumsum(reference_gaps, axis=1)
    scalars = jnp.concatenate(
        [
            jnp.broadcast_to(angular, (depths, 1)),
            references,
            references[:, 1:] - references[:, :-1],
        ],
        axis=1,
    )
    crosses = cross_spectra(
        devices, scalars, source_field[:, 0], receiver_field[:, 0], jnp.stack(windows),
        reference_index,
    )
    scale = frequency_bins.shape[0] ** (-0.5)
    return (
        jnp.einsum(
            "dwcab,cwl->dabl", crosses, lag_weights, preferred_element_type=jnp.float32
        )
        * scale
    )


def solution(mesh):
    placed = (
        P("grp", "freq", None, None),
        P("grp", "freq", None, None),
        P(("grp", "freq"), None, None),
        P("grp"),
        P("grp", None),
        P("grp", None, None),
        P(),
        P("grp"),
    )
    return jax.shard_map(
        functools.partial(shards, mesh.shape["freq"]),
        mesh=mesh,
        in_specs=placed,
        out_specs=P("grp", "freq", None, None),
        check_vma=False,
    )
```

```python
import functools
import math

import jax
import jax.numpy as jnp
import numpy as np
from jax import lax
from jax.experimental import pallas as pl
from jax.experimental.pallas import tpu as pltpu
from jax.sharding import PartitionSpec as P

LAGS = 256

cell_width = 0.0125
layer_thick = 0.0125
bin_hertz = 0.5
period_bins = 500
slow_base = 0.3
chunk = 16
tile = 256


def spectral_order(length):
    half = length // 2
    return np.concatenate([np.arange(half), [half], np.arange(length - 1, half, -1)])


def parts_of(length):
    steps = np.arange(length, dtype=np.int64)
    phases = np.mod(steps[:, None] * steps[None, :], length).astype(np.float32)
    angles = phases * np.float32(2.0 * math.pi / length)
    scale = np.float32(1.0 / math.sqrt(length))
    return np.cos(angles) * scale, np.sin(angles) * scale


def transform_block(length):
    cosine, sine = parts_of(length)
    return np.block([[cosine, -sine], [sine, cosine]]).astype(jnp.bfloat16)


def transform_pair(length):
    cosine, sine = parts_of(length)
    order = spectral_order(length)
    return (
        np.concatenate([cosine[order], sine[order]], axis=1).astype(jnp.bfloat16),
        np.concatenate([cosine[:, order], sine[:, order]], axis=1).astype(jnp.bfloat16),
    )


def lag_table(frequency_bins, lag_count):
    offsets = jnp.arange(lag_count, dtype=jnp.int32) - lag_count // 2
    cycles = jnp.mod(frequency_bins[:, None] * offsets[None, :], period_bins).astype(jnp.float32)
    angles = cycles * (2.0 * math.pi / period_bins)
    return jnp.stack([jnp.cos(angles), -jnp.sin(angles)]).astype(jnp.bfloat16)


def sin_cos(angle):
    turns = jnp.floor(angle * (2.0 / math.pi) + 0.5)
    rest = angle - turns * 1.5707855224609375
    rest = rest - turns * 1.0804334124e-05
    quarter = turns.astype(jnp.int32)
    square = rest * rest
    sine = rest + rest * square * (
        -1.6666654611e-1 + square * (8.3321608736e-3 + square * -1.9515295891e-4)
    )
    cosine = (
        1.0
        - 0.5 * square
        + square * square
        * (4.166664568298827e-2 + square * (-1.388731625493765e-3 + square * 2.443315711809948e-5))
    )
    odd = (quarter & 1) == 1
    sine_out = jnp.where(odd, cosine, sine)
    cosine_out = jnp.where(odd, sine, cosine)
    sine_out = jnp.where((quarter & 2) == 2, -sine_out, sine_out)
    cosine_out = jnp.where(((quarter + 1) & 2) == 2, -cosine_out, cosine_out)
    return sine_out, cosine_out


def window_kernel(
    devices, bins, gaps, source, receiver, table_f, table_i, table_y, windows, bracket,
    received,
    half, spectrum, shifted_a, shifted_b, returned, refocused, fields, cross,
    pair, part, parts, total, slow,
    pair_sems, scatter_sems, gather_sems, cross_sems,
):
    depths, rows_x, cols_y = bracket.shape
    chips = devices // 2
    me = lax.axis_index("freq")
    grp = lax.axis_index("grp")
    core = lax.rem(me, 2)
    chip = me // 2
    other = 1 - core
    share_rows = rows_x // devices
    signs = (1.0, -1.0)
    middle = rows_x // 2
    angular = bins[me].astype(jnp.float32) * (2.0 * math.pi * bin_hertz)
    references = []
    for d in range(depths):
        first = gaps[d, 0]
        second = first + gaps[d, 1]
        third = second + gaps[d, 2]
        references.append((slow_base + first, slow_base + second, slow_base + third))

    def lanes(which):
        return pl.ds(which * cols_y, cols_y)

    def remote(source_ref, target_ref, sems, place):
        return pltpu.make_async_remote_copy(
            src_ref=source_ref, dst_ref=target_ref, send_sem=sems[0], recv_sem=sems[1],
            device_id=(grp, place), device_id_type=pl.DeviceIdType.MESH,
        )

    def hop_to(hop):
        return lax.rem(chip + hop, chips)

    def swap_first(d):
        return remote(
            windows.at[d, other], pair.at[d], (pair_sems.at[d, 0], pair_sems.at[d, 1]),
            chip * 2 + other,
        )

    def scatter(d, hop):
        return remote(
            part.at[d, hop_to(hop)], parts.at[d, hop],
            (scatter_sems.at[d, 0, hop], scatter_sems.at[d, 1, hop]), hop_to(hop) * 2 + core,
        )

    def gather(d, hop):
        return remote(
            total.at[d], slow.at[d, core, chip],
            (gather_sems.at[d, 0, hop], gather_sems.at[d, 1, hop]), hop_to(hop) * 2 + core,
        )

    def swap_last(d):
        return remote(
            slow.at[d, core], slow.at[d, core], (pair_sems.at[d, 2], pair_sems.at[d, 3]),
            chip * 2 + other,
        )

    def send_cross(d, hop):
        to = lax.rem(me + hop, devices)
        return remote(
            cross.at[d, to], received.at[d, me],
            (cross_sems.at[d, 0, hop], cross_sems.at[d, 1, hop]), to,
        )

    def begin_scatter(d):
        swap_first(d).wait()
        part[d] = windows[d, core] + pair[d]

        @pl.loop(1, chips)
        def _(hop):
            scatter(d, hop).start()

    def begin_gather(d):
        @pl.loop(1, chips)
        def _(hop):
            scatter(d, hop).wait()

        summed = part[d, chip]
        for hop in range(1, chips):
            summed = summed + parts[d, hop]
        total[d] = summed
        slow[d, core, chip] = summed

        @pl.loop(1, chips)
        def _(hop):
            gather(d, hop).start()

    def begin_last(d):
        @pl.loop(1, chips)
        def _(hop):
            gather(d, hop).wait()

        swap_last(d).start()

    barrier = pltpu.get_barrier_semaphore()

    @pl.loop(1, devices)
    def _(hop):
        pl.semaphore_signal(
            barrier, inc=1, device_id=(grp, lax.rem(me + hop, devices)),
            device_id_type=pl.DeviceIdType.MESH,
        )

    pl.semaphore_wait(barrier, devices - 1)
    for d in range(depths):
        swap_first(d).start()

    columns = lax.broadcasted_iota(jnp.int32, (chunk, cols_y), 1)
    wave_y = jnp.where(columns < cols_y // 2, columns, cols_y - columns).astype(jnp.float32) * (
        2.0 * math.pi / (cols_y * cell_width)
    )
    squares_y = wave_y * wave_y

    def phases(d, ref, magnitude):
        wave_x = magnitude.astype(jnp.float32) * (2.0 * math.pi / (rows_x * cell_width))
        reach = angular * references[d][ref]
        radicand = reach * reach - (wave_x * wave_x + squares_y)
        depth = jnp.sqrt(jnp.abs(radicand)) * layer_thick
        moving = radicand > 0.0
        fading = jnp.exp(jnp.where(moving, 0.0, -depth))
        sine, cosine = sin_cos(jnp.where(moving, depth, 0.0) - reach * layer_thick)
        return fading * cosine, fading * sine

    def apply_phase(target, cosine, sine, start):
        rows = pl.ds(start, chunk)
        low_rows = pl.ds(rows_x + start, chunk)
        for which in range(2):
            turned = signs[which] * sine
            real = spectrum[rows, lanes(which)]
            imag = spectrum[low_rows, lanes(which)]
            new_real = (cosine * real - turned * imag).astype(jnp.bfloat16)
            target[rows, lanes(which)] = new_real
            target[low_rows, lanes(which)] = (-(cosine * imag + turned * real)).astype(jnp.bfloat16)
            target[pl.ds(2 * rows_x + start, chunk), lanes(which)] = -new_real

    counted = lax.broadcasted_iota(jnp.int32, (chunk, cols_y), 0)

    def shift_chunk(d, ref, target, start):
        cosine, sine = phases(d, ref, counted + start)
        apply_phase(target, cosine, sine, start)
        apply_phase(target, cosine, sine, pl.multiple_of(middle + start, chunk))

    def shift_edge(d, ref, target):
        cosine, sine = phases(d, ref, jnp.where(counted == 0, middle, counted))
        apply_phase(target, cosine, sine, middle)

    def multiply(table, values, rows):
        block = table[rows, :]
        real = jnp.dot(block, values[: 2 * rows_x, :], preferred_element_type=jnp.float32)
        imag = jnp.dot(block, values[rows_x:, :], preferred_element_type=jnp.float32)
        return real, imag

    def slow_rows(d, start):
        if share_rows >= chunk:
            block = start // share_rows
            inner = pl.multiple_of(lax.rem(start, share_rows), chunk)
            return slow[d, block // chips, lax.rem(block, chips), pl.ds(inner, chunk), :].astype(
                jnp.float32
            )
        pieces = []
        for piece in range(chunk // share_rows):
            block = start // share_rows + piece
            pieces.append(
                slow[d, block // chips, lax.rem(block, chips)].astype(jnp.float32)
            )
        return jnp.concatenate(pieces, axis=0)

    def store_cross(d, start, which, values):
        if share_rows >= chunk:
            inner = pl.multiple_of(lax.rem(start, share_rows), chunk)
            cross[d, start // share_rows, which, pl.ds(inner, chunk), :] = values.astype(
                jnp.bfloat16
            )
        else:
            for piece in range(chunk // share_rows):
                cross[d, start // share_rows + piece, which] = values[
                    piece * share_rows : (piece + 1) * share_rows
                ].astype(jnp.bfloat16)

    for d in range(depths):
        for which, field in enumerate((source, receiver) if d == 0 else (fields.at[0], fields.at[1])):
            for start in range(0, rows_x, tile):
                rows = pl.ds(start, tile)
                both = jnp.concatenate([field[0, rows, :], field[1, rows, :]], axis=1)
                out = jnp.dot(both, table_y[...], preferred_element_type=jnp.float32)
                out = out.astype(jnp.bfloat16)
                half[rows, lanes(which)] = out[:, :cols_y]
                half[pl.ds(rows_x + start, tile), lanes(which)] = out[:, cols_y:]
                half[pl.ds(2 * rows_x + start, tile), lanes(which)] = -out[:, :cols_y]
        if d == 0:
            begin_scatter(0)

        @pl.loop(0, rows_x // tile)
        def _(number):
            start = pl.multiple_of(number * tile, tile)
            real, imag = multiply(table_f, half, pl.ds(start, tile))
            spectrum[pl.ds(start, tile), :] = real
            spectrum[pl.ds(rows_x + start, tile), :] = imag

        if d == 0:
            begin_gather(0)
            for later in range(1, depths):
                begin_scatter(later)

        @pl.loop(0, middle // chunk)
        def _(number):
            shift_chunk(d, 0, shifted_a, pl.multiple_of(number * chunk, chunk))

        shift_edge(d, 0, shifted_a)
        for ref in range(3):
            now, later_shift = (shifted_a, shifted_b) if ref % 2 == 0 else (shifted_b, shifted_a)
            per_tile = middle // chunk // (rows_x // tile)

            @pl.loop(0, rows_x // tile)
            def _(number):
                start = pl.multiple_of(number * tile, tile)
                real, imag = multiply(table_i, now, pl.ds(start, tile))
                returned[pl.ds(start, tile), :] = real.astype(jnp.bfloat16)
                returned[pl.ds(rows_x + start, tile), :] = imag.astype(jnp.bfloat16)
                if ref < 2:
                    for each in range(per_tile):
                        shift_chunk(
                            d, ref + 1, later_shift,
                            pl.multiple_of((number * per_tile + each) * chunk, chunk),
                        )

            if ref < 2:
                shift_edge(d, ref + 1, later_shift)
            for which in range(2):
                for start in range(0, rows_x, tile):
                    rows = pl.ds(start, tile)
                    both = jnp.concatenate(
                        [
                            returned[rows, lanes(which)],
                            returned[pl.ds(rows_x + start, tile), lanes(which)],
                        ],
                        axis=1,
                    )
                    refocused[ref, which, rows, :] = jnp.dot(
                        both, table_y[...], preferred_element_type=jnp.float32
                    )
            if d == 0 and ref == 0:
                begin_last(0)
                for later in range(1, depths):
                    begin_gather(later)
            if d == 0 and ref == 1:
                for later in range(1, depths):
                    begin_last(later)
        if d == 0:
            for each in range(depths):
                swap_last(each).wait()

        @pl.loop(0, rows_x // chunk)
        def _(number):
            start = pl.multiple_of(number * chunk, chunk)
            rows = pl.ds(start, chunk)
            slowness = slow_rows(d, start)
            lower = bracket[d, rows, :] == 0
            slow_low = jnp.where(lower, references[d][0], references[d][1])
            slow_gap = jnp.where(
                lower, references[d][1] - references[d][0], references[d][2] - references[d][1]
            )
            weight = jnp.clip((slowness - slow_low) / slow_gap, 0.0, 1.0)
            sine, cosine = sin_cos((angular * layer_thick) * slowness)
            rounded = []
            for which in range(2):
                mixed = []
                for side in range(2):
                    first = refocused[0, which, rows, lanes(side)]
                    second = refocused[1, which, rows, lanes(side)]
                    third = refocused[2, which, rows, lanes(side)]
                    low = jnp.where(lower, first, second)
                    high = jnp.where(lower, second, third)
                    mixed.append((1.0 - weight) * low + weight * high)
                turned = signs[which] * sine
                real = (cosine * mixed[0] + turned * mixed[1]).astype(jnp.bfloat16)
                imag = (turned * mixed[0] - cosine * mixed[1]).astype(jnp.bfloat16)
                if d < depths - 1:
                    fields[which, 0, rows, :] = real
                    fields[which, 1, rows, :] = imag
                rounded.append((real.astype(jnp.float32), imag.astype(jnp.float32)))
            (sr, si), (rr, ri) = rounded
            store_cross(d, start, 0, sr * rr + si * ri)
            store_cross(d, start, 1, sr * ri - si * rr)

        @pl.loop(1, devices)
        def _(hop):
            send_cross(d, hop).start()

        received[d, me] = cross[d, me]
    for d in range(depths):
        @pl.loop(1, devices)
        def _(hop):
            send_cross(d, hop).wait()


def cross_spectra(devices, bins, gaps, source, receiver, windows, bracket):
    depths, rows_x, cols_y = bracket.shape
    chips = devices // 2
    share_rows = rows_x // devices
    table_f, table_i = transform_pair(rows_x)
    vmem = pl.BlockSpec(memory_space=pltpu.VMEM)
    flops = 16 * rows_x * (2 * rows_x + 2 * cols_y) * 2 * cols_y * depths
    dma = pltpu.SemaphoreType.DMA
    held = (depths, chips, share_rows, cols_y)
    return pl.pallas_call(
        functools.partial(window_kernel, devices),
        out_shape=jax.ShapeDtypeStruct((depths, devices, 2, share_rows, cols_y), jnp.bfloat16),
        in_specs=[pl.BlockSpec(memory_space=pltpu.SMEM)] * 2 + [vmem] * 7,
        out_specs=vmem,
        scratch_shapes=[
            pltpu.VMEM((3 * rows_x, 2 * cols_y), jnp.bfloat16),
            pltpu.VMEM((2 * rows_x, 2 * cols_y), jnp.float32),
            pltpu.VMEM((3 * rows_x, 2 * cols_y), jnp.bfloat16),
            pltpu.VMEM((3 * rows_x, 2 * cols_y), jnp.bfloat16),
            pltpu.VMEM((2 * rows_x, 2 * cols_y), jnp.bfloat16),
            pltpu.VMEM((3, 2, rows_x, 2 * cols_y), jnp.float32),
            pltpu.VMEM((2, 2, rows_x, cols_y), jnp.bfloat16),
            pltpu.VMEM((depths, devices, 2, share_rows, cols_y), jnp.bfloat16),
            pltpu.VMEM(held, jnp.bfloat16),
            pltpu.VMEM(held, jnp.bfloat16),
            pltpu.VMEM(held, jnp.bfloat16),
            pltpu.VMEM((depths, share_rows, cols_y), jnp.bfloat16),
            pltpu.VMEM((depths, 2, chips, share_rows, cols_y), jnp.bfloat16),
            dma((depths, 4)),
            dma((depths, 2, chips)),
            dma((depths, 2, chips)),
            dma((depths, 2, devices)),
        ],
        cost_estimate=pl.CostEstimate(
            flops=4 * flops, bytes_accessed=8 * 1024 * 1024, transcendentals=0
        ),
        compiler_params=pltpu.CompilerParams(
            collective_id=0, has_side_effects=True, vmem_limit_bytes=56 * 1024 * 1024
        ),
    )(
        bins, gaps, source, receiver, jnp.asarray(table_f), jnp.asarray(table_i),
        jnp.asarray(transform_block(cols_y)),
        windows.reshape(depths, 2, chips, share_rows, cols_y), bracket,
    )


def cut_kernel(slab_count, slab_map, corner, slab, out):
    owner = slab_map[pl.program_id(0)] // slab_count
    _, rows_x, cols_y = out.shape
    _, rows_all, cols_all = slab.shape
    held = lax.axis_index("freq")

    @pl.when(owner != held)
    def _():
        out[...] = jnp.zeros(out.shape, out.dtype)

    @pl.when(owner == held)
    def _():
        base = corner[0] // chunk * chunk
        up = lax.rem(2 * chunk - (corner[0] - base), 2 * chunk)
        left = lax.rem(cols_all - corner[1], cols_all)

        @pl.loop(0, rows_x // chunk)
        def _(number):
            start = pl.multiple_of(base + number * chunk, chunk)
            after = pl.multiple_of(jnp.minimum(start + chunk, rows_all - chunk), chunk)
            both = jnp.concatenate(
                [slab[0, pl.ds(start, chunk), :], slab[0, pl.ds(after, chunk), :]], axis=0
            ).astype(jnp.float32)
            both = pltpu.roll(both, up, 0)[:chunk]
            both = pltpu.roll(both, left, 1)[:, :cols_y]
            out[0, pl.ds(pl.multiple_of(number * chunk, chunk), chunk), :] = both.astype(out.dtype)


def cut_windows(slab_map, corner, slabs, rows_x, cols_y):
    slab_count, rows_all, cols_all = slabs.shape
    depths = slab_map.shape[0]
    return pl.pallas_call(
        functools.partial(cut_kernel, slab_count),
        out_shape=jax.ShapeDtypeStruct((depths, rows_x, cols_y), slabs.dtype),
        grid_spec=pltpu.PrefetchScalarGridSpec(
            num_scalar_prefetch=2,
            grid=(depths,),
            in_specs=[
                pl.BlockSpec(
                    (1, rows_all, cols_all),
                    lambda d, slab_map, corner: (lax.rem(slab_map[d], slab_count), 0, 0),
                )
            ],
            out_specs=pl.BlockSpec((1, rows_x, cols_y), lambda d, slab_map, corner: (d, 0, 0)),
        ),
    )(slab_map, corner, slabs)


def image_kernel(scale, crosses, weights, out):
    _, slots, _, rows, cols_y = crosses.shape
    values = crosses[0].astype(jnp.float32).reshape(2 * slots, rows, cols_y)
    values = jnp.swapaxes(values, 0, 1).astype(jnp.bfloat16)
    for row in range(rows):
        out[0, row] = scale * lax.dot_general(
            values[row], weights[...], (((0,), (0,)), ((), ())),
            preferred_element_type=jnp.float32,
        )


def lag_image(crosses, weights):
    depths, slots, _, rows, cols_y = crosses.shape
    lag_count = weights.shape[1]
    step = min(8, rows)
    return pl.pallas_call(
        functools.partial(image_kernel, slots ** (-0.5)),
        out_shape=jax.ShapeDtypeStruct((depths, rows, cols_y, lag_count), jnp.float32),
        grid=(depths, rows // step),
        in_specs=[
            pl.BlockSpec((1, slots, 2, step, cols_y), lambda d, r: (d, 0, 0, r, 0)),
            pl.BlockSpec((2 * slots, lag_count), lambda d, r: (0, 0)),
        ],
        out_specs=pl.BlockSpec((1, step, cols_y, lag_count), lambda d, r: (d, r, 0, 0)),
    )(crosses, weights)


def shards(
    devices,
    source_field,
    receiver_field,
    slowness_slabs,
    slab_map,
    reference_gaps,
    reference_index,
    frequency_bins,
    shot_corner,
):
    rows_x, cols_y = source_field.shape[2:]
    lag_weights = jnp.swapaxes(lag_table(frequency_bins, LAGS), 0, 1)
    windows = cut_windows(slab_map, shot_corner, slowness_slabs, rows_x, cols_y)
    crosses = cross_spectra(
        devices, frequency_bins, reference_gaps, source_field[:, 0], receiver_field[:, 0],
        windows, reference_index,
    )
    return lag_image(crosses, lag_weights.reshape(-1, LAGS))


def solution(mesh):
    placed = (
        P("grp", "freq", None, None),
        P("grp", "freq", None, None),
        P(("grp", "freq"), None, None),
        P("grp"),
        P("grp", None),
        P("grp", None, None),
        P(),
        P("grp"),
    )
    return jax.shard_map(
        functools.partial(shards, mesh.shape["freq"]),
        mesh=mesh,
        in_specs=placed,
        out_specs=P("grp", "freq", None, None),
        check_vma=False,
    )
```

```python
import functools
import math

import jax
import jax.numpy as jnp
import numpy as np
from jax import lax
from jax.experimental import pallas as pl
from jax.experimental.pallas import tpu as pltpu
from jax.sharding import PartitionSpec as P

LAGS = 256

cell_width = 0.0125
layer_thick = 0.0125
bin_hertz = 0.5
period_bins = 500
slow_base = 0.3
chunk = 16
tile = 256


def spectral_order(length):
    half = length // 2
    return np.concatenate([np.arange(half), [half], np.arange(length - 1, half, -1)])


def parts_of(length):
    steps = np.arange(length, dtype=np.int64)
    phases = np.mod(steps[:, None] * steps[None, :], length).astype(np.float32)
    angles = phases * np.float32(2.0 * math.pi / length)
    scale = np.float32(1.0 / math.sqrt(length))
    return np.cos(angles) * scale, np.sin(angles) * scale


def transform_block(length):
    cosine, sine = parts_of(length)
    return np.block([[cosine, -sine], [sine, cosine]]).astype(jnp.bfloat16)


def transform_pair(length):
    cosine, sine = parts_of(length)
    order = spectral_order(length)
    return (
        np.concatenate([cosine[order], sine[order]], axis=1).astype(jnp.bfloat16),
        np.concatenate([cosine[:, order], sine[:, order]], axis=1).astype(jnp.bfloat16),
    )


def lag_table(frequency_bins, lag_count):
    offsets = jnp.arange(lag_count, dtype=jnp.int32) - lag_count // 2
    cycles = jnp.mod(frequency_bins[:, None] * offsets[None, :], period_bins).astype(jnp.float32)
    angles = cycles * (2.0 * math.pi / period_bins)
    return jnp.stack([jnp.cos(angles), -jnp.sin(angles)]).astype(jnp.bfloat16)


def sin_cos(angle):
    turns = jnp.floor(angle * (2.0 / math.pi) + 0.5)
    rest = angle - turns * 1.5707855224609375
    rest = rest - turns * 1.0804334124e-05
    quarter = turns.astype(jnp.int32)
    square = rest * rest
    sine = rest + rest * square * (
        -1.6666654611e-1 + square * (8.3321608736e-3 + square * -1.9515295891e-4)
    )
    cosine = (
        1.0
        - 0.5 * square
        + square * square
        * (4.166664568298827e-2 + square * (-1.388731625493765e-3 + square * 2.443315711809948e-5))
    )
    odd = (quarter & 1) == 1
    sine_out = jnp.where(odd, cosine, sine)
    cosine_out = jnp.where(odd, sine, cosine)
    sine_out = jnp.where((quarter & 2) == 2, -sine_out, sine_out)
    cosine_out = jnp.where(((quarter + 1) & 2) == 2, -cosine_out, cosine_out)
    return sine_out, cosine_out


def window_kernel(
    devices, bins, gaps, source, receiver, table_f, table_i, table_y, windows, bracket,
    received,
    half, spectrum, shifted_a, shifted_b, shifted_c, returned, refocused, fields, cross,
    pair, part, parts, total, slow,
    pair_sems, scatter_sems, gather_sems, cross_sems,
):
    depths, rows_x, cols_y = bracket.shape
    chips = devices // 2
    me = lax.axis_index("freq")
    grp = lax.axis_index("grp")
    core = lax.rem(me, 2)
    chip = me // 2
    other = 1 - core
    share_rows = rows_x // devices
    signs = (1.0, -1.0)
    middle = rows_x // 2
    tiles = rows_x // tile
    group = max(share_rows, chunk)
    groups = tile // group
    shifted = (shifted_a, shifted_b, shifted_c)
    angular = bins[me].astype(jnp.float32) * (2.0 * math.pi * bin_hertz)
    references = []
    for d in range(depths):
        first = gaps[d, 0]
        second = first + gaps[d, 1]
        third = second + gaps[d, 2]
        references.append((slow_base + first, slow_base + second, slow_base + third))

    def lanes(which):
        return pl.ds(which * cols_y, cols_y)

    def remote(source_ref, target_ref, sems, place):
        return pltpu.make_async_remote_copy(
            src_ref=source_ref, dst_ref=target_ref, send_sem=sems[0], recv_sem=sems[1],
            device_id=(grp, place), device_id_type=pl.DeviceIdType.MESH,
        )

    def hop_to(hop):
        return lax.rem(chip + hop, chips)

    def swap_first(d):
        return remote(
            windows.at[d, other], pair.at[d], (pair_sems.at[d, 0], pair_sems.at[d, 1]),
            chip * 2 + other,
        )

    def scatter(d, hop):
        return remote(
            part.at[d, hop_to(hop)], parts.at[d, hop],
            (scatter_sems.at[d, 0, hop], scatter_sems.at[d, 1, hop]), hop_to(hop) * 2 + core,
        )

    def gather(d, hop):
        return remote(
            total.at[d], slow.at[d, core, chip],
            (gather_sems.at[d, 0, hop], gather_sems.at[d, 1, hop]), hop_to(hop) * 2 + core,
        )

    def swap_last(d):
        return remote(
            slow.at[d, core], slow.at[d, core], (pair_sems.at[d, 2], pair_sems.at[d, 3]),
            chip * 2 + other,
        )

    def send_cross(d, hop):
        to = lax.rem(me + hop, devices)
        return remote(
            cross.at[d, to], received.at[d, me],
            (cross_sems.at[d, 0, hop], cross_sems.at[d, 1, hop]), to,
        )

    def begin_scatter(d):
        swap_first(d).wait()
        part[d] = windows[d, core] + pair[d]

        @pl.loop(1, chips)
        def _(hop):
            scatter(d, hop).start()

    def begin_gather(d):
        @pl.loop(1, chips)
        def _(hop):
            scatter(d, hop).wait()

        summed = part[d, chip]
        for hop in range(1, chips):
            summed = summed + parts[d, hop]
        total[d] = summed
        slow[d, core, chip] = summed

        @pl.loop(1, chips)
        def _(hop):
            gather(d, hop).start()

    def begin_last(d):
        @pl.loop(1, chips)
        def _(hop):
            gather(d, hop).wait()

        swap_last(d).start()

    barrier = pltpu.get_barrier_semaphore()

    @pl.loop(1, devices)
    def _(hop):
        pl.semaphore_signal(
            barrier, inc=1, device_id=(grp, lax.rem(me + hop, devices)),
            device_id_type=pl.DeviceIdType.MESH,
        )

    pl.semaphore_wait(barrier, devices - 1)
    for d in range(depths):
        swap_first(d).start()

    columns = lax.broadcasted_iota(jnp.int32, (chunk, cols_y), 1)
    wave_y = jnp.where(columns < cols_y // 2, columns, cols_y - columns).astype(jnp.float32) * (
        2.0 * math.pi / (cols_y * cell_width)
    )
    squares_y = wave_y * wave_y

    def phases(d, ref, magnitude):
        wave_x = magnitude.astype(jnp.float32) * (2.0 * math.pi / (rows_x * cell_width))
        reach = angular * references[d][ref]
        radicand = reach * reach - (wave_x * wave_x + squares_y)
        depth = jnp.sqrt(jnp.abs(radicand)) * layer_thick
        moving = radicand > 0.0
        fading = jnp.exp(jnp.where(moving, 0.0, -depth))
        sine, cosine = sin_cos(jnp.where(moving, depth, 0.0) - reach * layer_thick)
        return fading * cosine, fading * sine

    def apply_phase(target, cosine, sine, start):
        rows = pl.ds(start, chunk)
        low_rows = pl.ds(rows_x + start, chunk)
        for which in range(2):
            turned = signs[which] * sine
            real = spectrum[rows, lanes(which)]
            imag = spectrum[low_rows, lanes(which)]
            new_real = (cosine * real - turned * imag).astype(jnp.bfloat16)
            target[rows, lanes(which)] = new_real
            target[low_rows, lanes(which)] = (-(cosine * imag + turned * real)).astype(jnp.bfloat16)
            target[pl.ds(2 * rows_x + start, chunk), lanes(which)] = -new_real

    counted = lax.broadcasted_iota(jnp.int32, (chunk, cols_y), 0)

    def shift_chunk(d, ref, target, start):
        cosine, sine = phases(d, ref, counted + start)
        apply_phase(target, cosine, sine, start)
        apply_phase(target, cosine, sine, pl.multiple_of(middle + start, chunk))

    def shift_edge(d, ref, target):
        cosine, sine = phases(d, ref, jnp.where(counted == 0, middle, counted))
        apply_phase(target, cosine, sine, middle)

    def multiply(table, values, rows):
        block = table[rows, :]
        real = jnp.dot(block, values[: 2 * rows_x, :], preferred_element_type=jnp.float32)
        imag = jnp.dot(block, values[rows_x:, :], preferred_element_type=jnp.float32)
        return real, imag

    def slow_rows(d, start):
        if share_rows >= chunk:
            block = start // share_rows
            inner = pl.multiple_of(lax.rem(start, share_rows), chunk)
            return slow[d, block // chips, lax.rem(block, chips), pl.ds(inner, chunk), :].astype(
                jnp.float32
            )
        pieces = []
        for piece in range(chunk // share_rows):
            block = start // share_rows + piece
            pieces.append(
                slow[d, block // chips, lax.rem(block, chips)].astype(jnp.float32)
            )
        return jnp.concatenate(pieces, axis=0)

    def store_cross(d, start, which, values):
        if share_rows >= chunk:
            inner = pl.multiple_of(lax.rem(start, share_rows), chunk)
            cross[d, start // share_rows, which, pl.ds(inner, chunk), :] = values.astype(
                jnp.bfloat16
            )
        else:
            for piece in range(chunk // share_rows):
                cross[d, start // share_rows + piece, which] = values[
                    piece * share_rows : (piece + 1) * share_rows
                ].astype(jnp.bfloat16)

    def mix(d, inside, start):
        local = pl.ds(inside, chunk)
        rows = pl.ds(start, chunk)
        slowness = slow_rows(d, start)
        lower = bracket[d, rows, :] == 0
        slow_low = jnp.where(lower, references[d][0], references[d][1])
        slow_gap = jnp.where(
            lower, references[d][1] - references[d][0], references[d][2] - references[d][1]
        )
        weight = jnp.clip((slowness - slow_low) / slow_gap, 0.0, 1.0)
        sine, cosine = sin_cos((angular * layer_thick) * slowness)
        rounded = []
        for which in range(2):
            mixed = []
            for side in range(2):
                first = refocused[0, which, local, lanes(side)]
                second = refocused[1, which, local, lanes(side)]
                third = refocused[2, which, local, lanes(side)]
                low = jnp.where(lower, first, second)
                high = jnp.where(lower, second, third)
                mixed.append((1.0 - weight) * low + weight * high)
            turned = signs[which] * sine
            real = (cosine * mixed[0] + turned * mixed[1]).astype(jnp.bfloat16)
            imag = (turned * mixed[0] - cosine * mixed[1]).astype(jnp.bfloat16)
            if d < depths - 1:
                fields[which, 0, rows, :] = real
                fields[which, 1, rows, :] = imag
            rounded.append((real.astype(jnp.float32), imag.astype(jnp.float32)))
        (sr, si), (rr, ri) = rounded
        store_cross(d, start, 0, sr * rr + si * ri)
        store_cross(d, start, 1, sr * ri - si * rr)

    for d in range(depths):
        for which, field in enumerate((source, receiver) if d == 0 else (fields.at[0], fields.at[1])):
            for start in range(0, rows_x, tile):
                rows = pl.ds(start, tile)
                both = jnp.concatenate([field[0, rows, :], field[1, rows, :]], axis=1)
                out = jnp.dot(both, table_y[...], preferred_element_type=jnp.float32)
                out = out.astype(jnp.bfloat16)
                half[rows, lanes(which)] = out[:, :cols_y]
                half[pl.ds(rows_x + start, tile), lanes(which)] = out[:, cols_y:]
                half[pl.ds(2 * rows_x + start, tile), lanes(which)] = -out[:, :cols_y]
        if d == 0:
            begin_scatter(0)

        @pl.loop(0, rows_x // tile)
        def _(number):
            start = pl.multiple_of(number * tile, tile)
            real, imag = multiply(table_f, half, pl.ds(start, tile))
            spectrum[pl.ds(start, tile), :] = real
            spectrum[pl.ds(rows_x + start, tile), :] = imag

        if d == 0:
            begin_gather(0)
            for later in range(1, depths):
                begin_scatter(later)

        @pl.loop(0, middle // chunk)
        def _(number):
            shift_chunk(d, 0, shifted[0], pl.multiple_of(number * chunk, chunk))

        shift_edge(d, 0, shifted[0])
        own_tile = me * share_rows // tile
        own_group = lax.rem(me * share_rows, tile) // group
        for turn in range(tiles):
            tile_start = pl.multiple_of(lax.rem(own_tile + 1 + turn, tiles) * tile, tile)
            for ref in range(3):
                if turn == 0 and ref < 2:
                    part_rows = tile // 2

                    @pl.loop(0, 2)
                    def _(side):
                        inner = pl.multiple_of(side * part_rows, part_rows)
                        real, imag = multiply(
                            table_i, shifted[ref], pl.ds(tile_start + inner, part_rows)
                        )
                        returned[pl.ds(inner, part_rows), :] = real.astype(jnp.bfloat16)
                        returned[pl.ds(tile + inner, part_rows), :] = imag.astype(jnp.bfloat16)
                        for each in range(middle // chunk // 2):
                            shift_chunk(
                                d, ref + 1, shifted[ref + 1],
                                pl.multiple_of(side * (middle // 2) + each * chunk, chunk),
                            )

                    shift_edge(d, ref + 1, shifted[ref + 1])
                else:
                    real, imag = multiply(table_i, shifted[ref], pl.ds(tile_start, tile))
                    returned[:tile, :] = real.astype(jnp.bfloat16)
                    returned[tile:, :] = imag.astype(jnp.bfloat16)
                for which in range(2):
                    both = jnp.concatenate(
                        [returned[:tile, lanes(which)], returned[tile:, lanes(which)]], axis=1
                    )
                    refocused[ref, which] = jnp.dot(
                        both, table_y[...], preferred_element_type=jnp.float32
                    )
                if d == 0 and turn == 0 and ref == 0:
                    begin_last(0)
                if d == 0 and turn == 0 and ref == 1:
                    for later in range(1, depths):
                        begin_gather(later)
                if d == 0 and turn == tiles - 1 and ref == 1:
                    for later in range(1, depths):
                        begin_last(later)
            if d == 0 and turn == 0:
                swap_last(0).wait()

            def send_group(index):
                for each in range(group // share_rows):
                    to = (tile_start + index * group) // share_rows + each
                    hop = lax.rem(to - me + devices, devices)

                    @pl.when(hop != 0)
                    def _():
                        send_cross(d, hop).start()

            def turn_index(number):
                return lax.rem(own_group + 1 + number, groups)

            @pl.loop(0, groups)
            def _(number):
                for each in range(group // chunk):
                    inside = pl.multiple_of(turn_index(number) * group + each * chunk, chunk)
                    mix(d, inside, pl.multiple_of(tile_start + inside, chunk))

                @pl.when(number > 0)
                def _():
                    send_group(turn_index(number - 1))

            send_group(turn_index(groups - 1))

        if d == 0:
            for later in range(1, depths):
                swap_last(later).wait()
        received[d, me] = cross[d, me]
    for d in range(depths):
        @pl.loop(1, devices)
        def _(hop):
            send_cross(d, hop).wait()


def cross_spectra(devices, bins, gaps, source, receiver, windows, bracket):
    depths, rows_x, cols_y = bracket.shape
    chips = devices // 2
    share_rows = rows_x // devices
    table_f, table_i = transform_pair(rows_x)
    vmem = pl.BlockSpec(memory_space=pltpu.VMEM)
    flops = 16 * rows_x * (2 * rows_x + 2 * cols_y) * 2 * cols_y * depths
    dma = pltpu.SemaphoreType.DMA
    held = (depths, chips, share_rows, cols_y)
    return pl.pallas_call(
        functools.partial(window_kernel, devices),
        out_shape=jax.ShapeDtypeStruct((depths, devices, 2, share_rows, cols_y), jnp.bfloat16),
        in_specs=[pl.BlockSpec(memory_space=pltpu.SMEM)] * 2 + [vmem] * 7,
        out_specs=vmem,
        scratch_shapes=[
            pltpu.VMEM((3 * rows_x, 2 * cols_y), jnp.bfloat16),
            pltpu.VMEM((2 * rows_x, 2 * cols_y), jnp.float32),
            pltpu.VMEM((3 * rows_x, 2 * cols_y), jnp.bfloat16),
            pltpu.VMEM((3 * rows_x, 2 * cols_y), jnp.bfloat16),
            pltpu.VMEM((3 * rows_x, 2 * cols_y), jnp.bfloat16),
            pltpu.VMEM((2 * tile, 2 * cols_y), jnp.bfloat16),
            pltpu.VMEM((3, 2, tile, 2 * cols_y), jnp.float32),
            pltpu.VMEM((2, 2, rows_x, cols_y), jnp.bfloat16),
            pltpu.VMEM((depths, devices, 2, share_rows, cols_y), jnp.bfloat16),
            pltpu.VMEM(held, jnp.bfloat16),
            pltpu.VMEM(held, jnp.bfloat16),
            pltpu.VMEM(held, jnp.bfloat16),
            pltpu.VMEM((depths, share_rows, cols_y), jnp.bfloat16),
            pltpu.VMEM((depths, 2, chips, share_rows, cols_y), jnp.bfloat16),
            dma((depths, 4)),
            dma((depths, 2, chips)),
            dma((depths, 2, chips)),
            dma((depths, 2, devices)),
        ],
        cost_estimate=pl.CostEstimate(
            flops=4 * flops, bytes_accessed=8 * 1024 * 1024, transcendentals=0
        ),
        compiler_params=pltpu.CompilerParams(
            collective_id=0, has_side_effects=True, vmem_limit_bytes=56 * 1024 * 1024
        ),
    )(
        bins, gaps, source, receiver, jnp.asarray(table_f), jnp.asarray(table_i),
        jnp.asarray(transform_block(cols_y)),
        windows.reshape(depths, 2, chips, share_rows, cols_y), bracket,
    )


def cut_kernel(slab_count, slab_map, corner, slab, out):
    owner = slab_map[pl.program_id(0)] // slab_count
    _, rows_x, cols_y = out.shape
    _, rows_all, cols_all = slab.shape
    held = lax.axis_index("freq")

    @pl.when(owner != held)
    def _():
        out[...] = jnp.zeros(out.shape, out.dtype)

    @pl.when(owner == held)
    def _():
        base = corner[0] // chunk * chunk
        up = lax.rem(2 * chunk - (corner[0] - base), 2 * chunk)
        left = lax.rem(cols_all - corner[1], cols_all)

        @pl.loop(0, rows_x // chunk)
        def _(number):
            start = pl.multiple_of(base + number * chunk, chunk)
            after = pl.multiple_of(jnp.minimum(start + chunk, rows_all - chunk), chunk)
            both = jnp.concatenate(
                [slab[0, pl.ds(start, chunk), :], slab[0, pl.ds(after, chunk), :]], axis=0
            ).astype(jnp.float32)
            both = pltpu.roll(both, up, 0)[:chunk]
            both = pltpu.roll(both, left, 1)[:, :cols_y]
            out[0, pl.ds(pl.multiple_of(number * chunk, chunk), chunk), :] = both.astype(out.dtype)


def cut_windows(slab_map, corner, slabs, rows_x, cols_y):
    slab_count, rows_all, cols_all = slabs.shape
    depths = slab_map.shape[0]
    return pl.pallas_call(
        functools.partial(cut_kernel, slab_count),
        out_shape=jax.ShapeDtypeStruct((depths, rows_x, cols_y), slabs.dtype),
        grid_spec=pltpu.PrefetchScalarGridSpec(
            num_scalar_prefetch=2,
            grid=(depths,),
            in_specs=[
                pl.BlockSpec(
                    (1, rows_all, cols_all),
                    lambda d, slab_map, corner: (lax.rem(slab_map[d], slab_count), 0, 0),
                )
            ],
            out_specs=pl.BlockSpec((1, rows_x, cols_y), lambda d, slab_map, corner: (d, 0, 0)),
        ),
    )(slab_map, corner, slabs)


def image_kernel(scale, crosses, weights, out):
    _, slots, _, rows, cols_y = crosses.shape
    values = crosses[0].astype(jnp.float32).reshape(2 * slots, rows, cols_y)
    values = jnp.swapaxes(values, 0, 1).astype(jnp.bfloat16)
    for row in range(rows):
        out[0, row] = scale * lax.dot_general(
            values[row], weights[...], (((0,), (0,)), ((), ())),
            preferred_element_type=jnp.float32,
        )


def lag_image(crosses, weights):
    depths, slots, _, rows, cols_y = crosses.shape
    lag_count = weights.shape[1]
    step = min(8, rows)
    return pl.pallas_call(
        functools.partial(image_kernel, slots ** (-0.5)),
        out_shape=jax.ShapeDtypeStruct((depths, rows, cols_y, lag_count), jnp.float32),
        grid=(depths, rows // step),
        in_specs=[
            pl.BlockSpec((1, slots, 2, step, cols_y), lambda d, r: (d, 0, 0, r, 0)),
            pl.BlockSpec((2 * slots, lag_count), lambda d, r: (0, 0)),
        ],
        out_specs=pl.BlockSpec((1, step, cols_y, lag_count), lambda d, r: (d, r, 0, 0)),
    )(crosses, weights)


def shards(
    devices,
    source_field,
    receiver_field,
    slowness_slabs,
    slab_map,
    reference_gaps,
    reference_index,
    frequency_bins,
    shot_corner,
):
    rows_x, cols_y = source_field.shape[2:]
    lag_weights = jnp.swapaxes(lag_table(frequency_bins, LAGS), 0, 1)
    windows = cut_windows(slab_map, shot_corner, slowness_slabs, rows_x, cols_y)
    crosses = cross_spectra(
        devices, frequency_bins, reference_gaps, source_field[:, 0], receiver_field[:, 0],
        windows, reference_index,
    )
    return lag_image(crosses, lag_weights.reshape(-1, LAGS))


def solution(mesh):
    placed = (
        P("grp", "freq", None, None),
        P("grp", "freq", None, None),
        P(("grp", "freq"), None, None),
        P("grp"),
        P("grp", None),
        P("grp", None, None),
        P(),
        P("grp"),
    )
    return jax.shard_map(
        functools.partial(shards, mesh.shape["freq"]),
        mesh=mesh,
        in_specs=placed,
        out_specs=P("grp", "freq", None, None),
        check_vma=False,
    )
```
